32 devices in a mesh: seq: 16 (over z, x, core), head: 2 (over y).
Axes of the slice: x: 2, y: 2, z: 4, core: 2. Of those that a mesh axis runs over, the one named last changes fastest.
Arguments:
- byte_rows: bfloat16 [16384, 1024], P('seq', 'head'), may hold values from -6 to 6
- pool_weight: bfloat16 [4, 1024, 1024], P(None, 'head'), may hold values from -0.09375 to 0.09375
- norm_gain: float32 [1024], replicated, may hold values from 0.1 to 1.9
- qkv_weight: bfloat16 [1024, 8, 3, 128], P(None, 'head')
- span_order: int32 [16], replicated, may hold values from 0 to 15, as said below
- query_start: int32 [1], replicated, may hold values from 2560 to 3072
Outputs:
- shortened: bfloat16 [4096, 1024], P('seq', 'head')
- context: bfloat16 [1024, 1024], P('seq', 'head')
- row_highest: float32 [8, 1024], P('head', 'seq')
The draws below stay inside these ranges and needn't reach their ends.
Inputs may be any that keep to these rules, and one draw needn't show every extreme that they name: `span_order`: entry i is (i + r) mod 16 for one r of each draw.
All inputs are finite; a program needn't handle non-finite values.
Results may differ from the reference program's by a relative error of at most 0.015.
Values may be sent and summed in bfloat16 or wider, within the bound.
A program may use at most 64 MiB of HBM per device.

```python
import jax
import jax.numpy as jnp
from jax import lax

D = 1024
HEADS = 8
HEAD_DIM = 128
SF = 4
SPAN = 128
PAIRS = 16
SHORT = 4096
BYTES = 16384
QUERIES = 1024


def draw_span_order(key, part):
    rotation = jax.random.randint(key, (), 0, PAIRS)
    return ((jnp.arange(PAIRS, dtype=jnp.int32) + rotation) % PAIRS).astype(jnp.int32)


def draw_qkv_weight(key, part):
    key_query, key_key, key_value = jax.random.split(jax.random.fold_in(key, 11), 3)
    spread = D ** (-0.5)
    query_part = jax.random.normal(key_query, (D, HEADS, 1, HEAD_DIM), jnp.float32) * spread
    value_part = jax.random.normal(key_value, (D, HEADS, 1, HEAD_DIM), jnp.float32) * spread
    noise_part = jax.random.normal(key_key, (D, HEADS, 1, HEAD_DIM), jnp.float32) * spread
    key_part = noise_part
    return jnp.concatenate([query_part, key_part, value_part], axis=2).astype(jnp.bfloat16)


def levels(key, extent, pieces, least, top_value):
    factor_of, own = 1.0, jax.random.fold_in(key, 6)
    for axis_at, shards_of in pieces:
        steps = jnp.exp(jax.random.uniform(jax.random.fold_in(own, axis_at), (shards_of,), jnp.float32, least / len(pieces), top_value / len(pieces)))
        factor_of = factor_of * jnp.repeat(steps, extent[axis_at] // shards_of).reshape([-1 if axis == axis_at else 1 for axis in range(len(extent))])
    return factor_of


def bell_draw(key, shape, scale, most, cuts=(), kind=jnp.bfloat16):
    factor_of = levels(key, shape, cuts, -0.22, 0.18) if cuts else 1.0
    drawn = jax.random.normal(key, shape, jnp.float32) * scale * factor_of
    return jnp.minimum(jnp.maximum(drawn, -most), most).astype(kind)


def setup_inputs(seed: int = 0) -> dict:
    streams_of = jax.random.split(jax.random.key(seed), 7)
    return {
        "byte_rows": bell_draw(streams_of[0], (BYTES, D), 1.0, 6.0, ((0, 16), (1, 2))),
        "pool_weight": bell_draw(streams_of[1], (SF, D, D), (SF * D) ** -0.5, 0.09375, ((1, 2),)),
        "norm_gain": jnp.clip(1.0 + 0.18 * jax.random.normal(streams_of[2], (D,), jnp.float32), 0.1, 1.9),
        "qkv_weight": draw_qkv_weight(jax.random.fold_in(streams_of[6], 71), 0),
        "span_order": draw_span_order(jax.random.fold_in(streams_of[6], 71), 0),
        "query_start": jax.random.randint(streams_of[5], (1,), SHORT - QUERIES - SHORT // 8, SHORT - QUERIES + 1).astype(jnp.int32),
    }


norm_epsilon = 1e-06
masked_score = -1e+30

def reference(byte_rows, pool_weight, norm_gain, qkv_weight, span_order, query_start):
    pair_count = PAIRS
    span_bytes = SF * SPAN
    pair_slots = jnp.arange(pair_count, dtype=jnp.int32)
    holder = jnp.zeros((pair_count,), jnp.int32).at[span_order].set(pair_slots)
    stored = byte_rows.reshape(pair_count, 2, span_bytes, D)
    ordered = jnp.concatenate([stored[holder, 0], stored[holder[::-1], 1]], axis=0).reshape(BYTES, D)
    shifted = jnp.concatenate([jnp.zeros((SF - 1, D), byte_rows.dtype), ordered[:BYTES - (SF - 1)]], axis=0)
    grouped = shifted.reshape(SHORT, SF * D)
    pooled = jnp.dot(grouped, pool_weight.reshape(SF * D, D), preferred_element_type=jnp.float32).astype(jnp.bfloat16)
    widened = pooled.astype(jnp.float32)
    squares = lax.optimization_barrier(jnp.sum(widened * widened, axis=1, keepdims=True)) / D
    normed = (widened * lax.rsqrt(squares + norm_epsilon) * norm_gain).astype(jnp.bfloat16)
    projected = jnp.dot(normed, qkv_weight.reshape(D, HEADS * 3 * HEAD_DIM), preferred_element_type=jnp.float32)
    projected = projected.astype(jnp.bfloat16).reshape(SHORT, HEADS, 3, HEAD_DIM)
    window_start = query_start[0].astype(jnp.int32)
    queries = lax.dynamic_slice_in_dim(projected[:, :, 0], window_start, QUERIES, 0).astype(jnp.float32)
    key_rows = projected[:, :, 1].astype(jnp.float32)
    value_rows = projected[:, :, 2].astype(jnp.float32)
    key_pos = jnp.arange(SHORT, dtype=jnp.int32)
    score_scale = HEAD_DIM ** (-0.5)
    step_rows = min(256, QUERIES)

    def attend(block_index):
        query_block = lax.dynamic_slice_in_dim(queries, (block_index * step_rows).astype(jnp.int32), step_rows, 0)
        query_pos = window_start + block_index * step_rows + jnp.arange(step_rows, dtype=jnp.int32)
        scores = jnp.einsum('qhd,khd->hqk', query_block, key_rows) * score_scale
        scores = jnp.where(key_pos[None, None, :] <= query_pos[None, :, None], scores, masked_score)
        highest = lax.optimization_barrier(jnp.max(scores, axis=2, keepdims=True))
        rounded = lax.optimization_barrier(jnp.exp(scores - highest).astype(jnp.bfloat16))
        weights = rounded.astype(jnp.float32)
        totals = lax.optimization_barrier(jnp.sum(weights, axis=2))
        summed = jnp.einsum('hqk,khd->qhd', weights, value_rows)
        return ((summed / totals.T[:, :, None]).astype(jnp.bfloat16), highest[:, :, 0])
    context, maxima = lax.map(attend, jnp.arange(QUERIES // step_rows, dtype=jnp.int32))
    context = context.reshape(QUERIES, D)
    row_highest = jnp.transpose(maxima, (1, 0, 2)).reshape(HEADS, QUERIES) * HEAD_DIM ** 0.5
    placed_ids = jnp.stack([span_order, 2 * pair_count - 1 - span_order], axis=1).reshape(2 * pair_count).astype(jnp.int32)
    shortened = pooled.reshape(2 * pair_count, SPAN, D)[placed_ids].reshape(SHORT, D)
    return (shortened, context, row_highest)
```

```python
import jax
import jax.numpy as jnp
import functools
from jax import lax
from jax.experimental import pallas as pl
from jax.experimental.pallas import tpu as pltpu
from jax.sharding import PartitionSpec as P

SF = 4
QROWS_DEV = 64


norm_epsilon = 1e-06
masked_score = -1e30


def extended(block, sides, width):
    for axis, dim in sides:
        count = lax.axis_size(axis)
        forward = [(i, i + 1) for i in range(count - 1)]
        forward.append((count - 1, 0))
        backward = [(target, source) for source, target in forward]
        low = lax.ppermute(
            lax.slice_in_dim(block, block.shape[dim] - width, None, axis=dim), axis, forward
        )
        high = lax.ppermute(lax.slice_in_dim(block, 0, width, axis=dim), axis, backward)
        block = jnp.concatenate([low, block, high], axis=dim)
    return block


def attend_kernel(place_ref, q_ref, k_ref, v_ref, o_ref, m_ref, l_ref, *, scale, span_rows):
    first_pos, second_pos, window_start = place_ref[0], place_ref[1], place_ref[2]
    keys, queries = k_ref.shape[0], q_ref.shape[0]
    scores = lax.dot_general(
        k_ref[...], q_ref[...], (((1,), (1,)), ((), ())), preferred_element_type=jnp.float32
    ) * scale
    row = lax.broadcasted_iota(jnp.int32, (keys, 1), 0)
    key_pos = jnp.where(row < span_rows, first_pos + row, second_pos + row - span_rows)
    query_pos = window_start + lax.broadcasted_iota(jnp.int32, (1, queries), 1)
    scores = jnp.where(key_pos <= query_pos, scores, masked_score)
    highest = jnp.max(scores, axis=0, keepdims=True)
    weights = jnp.exp(scores - highest).astype(jnp.bfloat16)
    m_ref[...] = highest[None]
    l_ref[...] = jnp.sum(weights.astype(jnp.float32), axis=0, keepdims=True)[None]
    o_ref[...] = lax.dot_general(
        weights, v_ref[...], (((0,), (0,)), ((), ())), preferred_element_type=jnp.float32
    ).astype(o_ref.dtype)


def attend_local(place, queries, projected, heads, head_width, span_rows):
    count, keys = queries.shape[0], projected.shape[0]
    stat = jax.ShapeDtypeStruct((heads, 1, count), jnp.float32)
    stat_spec = pl.BlockSpec((1, 1, count), lambda h, place: (h, 0, 0))
    return pl.pallas_call(
        functools.partial(attend_kernel, scale=head_width ** (-0.5), span_rows=span_rows),
        grid_spec=pltpu.PrefetchScalarGridSpec(
            num_scalar_prefetch=1,
            grid=(heads,),
            in_specs=[
                pl.BlockSpec((count, head_width), lambda h, place: (0, h)),
                pl.BlockSpec((keys, head_width), lambda h, place: (0, h * 3 + 1)),
                pl.BlockSpec((keys, head_width), lambda h, place: (0, h * 3 + 2)),
            ],
            out_specs=[
                pl.BlockSpec((count, head_width), lambda h, place: (0, h)),
                stat_spec,
                stat_spec,
            ],
        ),
        out_shape=[jax.ShapeDtypeStruct((count, heads * head_width), jnp.bfloat16), stat, stat],
    )(place, queries, projected, projected)


def gather_queries(own):
    return lax.all_gather(own, "seq", axis=0, tiled=False)


def exchange(parts, stats):
    parts = lax.all_to_all(parts, "seq", split_axis=0, concat_axis=0, tiled=True)
    stats = lax.all_to_all(stats, "seq", split_axis=0, concat_axis=0, tiled=True)
    return parts, stats


def body(byte_rows, pool_weight, norm_gain, qkv_weight, span_order, query_start):
    local_rows, features = byte_rows.shape
    half_rows = local_rows // 2
    short_rows = local_rows // SF
    span_rows = short_rows // 2
    model_width = qkv_weight.shape[0]
    heads_here = qkv_weight.shape[1]
    head_width = qkv_weight.shape[3]
    pair_count = lax.axis_size("seq")
    seq_index = lax.axis_index("seq")
    head_index = lax.axis_index("head")
    pair_slots = jnp.arange(pair_count, dtype=jnp.int32)
    my_pair = jnp.sum(jnp.where(pair_slots == seq_index, span_order, 0))
    shift_rows = SF - 1
    first_tail = byte_rows[half_rows - shift_rows : half_rows]
    outgoing = jnp.concatenate([byte_rows[local_rows - shift_rows :], first_tail], axis=0)
    padded = extended(outgoing, (("seq", 0),), shift_rows)
    from_before = padded[:shift_rows]
    from_after = padded[padded.shape[0] - shift_rows :]
    first_prev = jnp.where(my_pair == 0, jnp.zeros_like(from_before), from_before)
    second_prev = jnp.where(my_pair == pair_count - 1, first_tail, from_after)
    grouped = jnp.concatenate(
        [
            first_prev,
            byte_rows[: half_rows - shift_rows],
            second_prev,
            byte_rows[half_rows : local_rows - shift_rows],
        ],
        axis=0,
    )
    grouped = grouped.reshape(short_rows, SF * features)
    partial_value = jnp.dot(
        grouped, pool_weight.reshape(SF * features, model_width), preferred_element_type=jnp.float32
    )
    qkv_flat = qkv_weight.reshape(model_width, heads_here * 3 * head_width)
    if lax.axis_size("head") == 2:
        other = lax.ppermute(partial_value.astype(jnp.bfloat16), "head", [(0, 1), (1, 0)])
        pooled = (partial_value + other.astype(jnp.float32)).astype(jnp.bfloat16)
    else:
        pooled = lax.psum(partial_value, "head").astype(jnp.bfloat16)
    shortened = lax.dynamic_slice_in_dim(pooled, head_index * features, features, 1)
    widened = pooled.astype(jnp.float32)
    squares = jnp.sum(widened * widened, axis=1, keepdims=True) / model_width
    normed = (widened * lax.rsqrt(squares + norm_epsilon) * norm_gain).astype(jnp.bfloat16)
    projected = jnp.dot(normed, qkv_flat, preferred_element_type=jnp.float32).astype(jnp.bfloat16)
    query_total = QROWS_DEV * pair_count
    window_start = query_start[0]
    own_queries = projected[span_rows:].reshape(span_rows, heads_here, 3, head_width)[:, :, 0]
    own_queries = own_queries.reshape(span_rows, heads_here * head_width)
    gathered = gather_queries(own_queries)[::-1].reshape(-1, heads_here * head_width)
    start = span_order[0] * span_rows + window_start - pair_count * span_rows
    queries = lax.dynamic_slice_in_dim(
        jnp.concatenate([gathered, gathered], axis=0), start, query_total, 0
    )
    place = jnp.stack(
        [my_pair * span_rows, (2 * pair_count - 1 - my_pair) * span_rows, window_start]
    ).astype(jnp.int32)
    parts, highest, totals = attend_local(
        place, queries, projected, heads_here, head_width, span_rows
    )
    stats = jnp.stack([highest[:, 0], totals[:, 0]]).reshape(
        2 * heads_here, pair_count, QROWS_DEV
    )
    parts, stats = exchange(
        parts.reshape(pair_count, QROWS_DEV, heads_here * head_width), stats.transpose(1, 0, 2)
    )
    highs, sums = stats[:, :heads_here], stats[:, heads_here:]
    top = jnp.max(highs, axis=0)
    factor = jnp.exp(highs - top)
    total = jnp.sum(factor * sums, axis=0)
    share = (factor / total).transpose(0, 2, 1)
    context = jnp.concatenate(
        [
            jnp.sum(
                parts[:, :, h * head_width : (h + 1) * head_width].astype(jnp.float32)
                * share[:, :, h : h + 1],
                axis=0,
            )
            for h in range(heads_here)
        ],
        axis=1,
    )
    return shortened, context.astype(jnp.bfloat16), top * head_width**0.5


def solution(mesh):
    placed = (P("seq", "head"), P(None, "head", None), P(), P(None, "head", None, None), P(), P())
    return jax.shard_map(
        body,
        mesh=mesh,
        in_specs=placed,
        out_specs=(P("seq", "head"), P("seq", "head"), P("head", "seq")),
        check_vma=False,
    )
```
